32 devices in a mesh: groups: 2 (over x), ctx: 16 (over z, y, core).
Axes of the slice: x: 2, y: 2, z: 4, core: 2. Of those that a mesh axis runs over, the one named last changes fastest.
Arguments:
- queries: bfloat16 [8192, 1024], P(('groups', 'ctx')), parts along dimension 0, may hold values from -128 to 128
- keys: bfloat16 [8192, 128], P(('groups', 'ctx')), parts along dimension 0, may hold values from -32 to 32
- values: bfloat16 [8192, 128], P(('groups', 'ctx')), parts along dimension 0, may hold values from -6 to 6
- doc_ids: int32 [8192], P(('groups', 'ctx')), parts along dimension 0, may hold values from 0 to 2, never falling along the last dimension, each value on 1 to 3072 neighbouring positions
Outputs:
- attended: bfloat16 [8192, 1024], P(('groups', 'ctx')), parts along dimension 0
The draws below stay inside these ranges and needn't reach their ends.
There are 2 independent parts, one for each index of `groups`. The reference program is written for one: setup_inputs(seed, part) draws one part's arguments, and reference() takes and returns one part's arrays. A program takes and returns all parts, laid end to end along the dimension named above; each array names one. Nothing has to cross between parts.
All inputs are finite; a program needn't handle non-finite values.
Results may differ from the reference program's by a relative error of at most 0.0041.
Values may be sent and summed in bfloat16 or wider, within the bound.
No kernel may reach another device: no remote copies, remote signals or barrier semaphores. Data moves between devices by JAX's collectives and lax.ppermute only.
A program may use at most 64 MiB of HBM per device.

```python
import math
import jax
import jax.numpy as jnp
import numpy as np
from jax import lax

HEADS = 8
HEAD_DIM = 128
DOCS = 3
HALF = 128
SEQ = 4096
LONGEST = 3072


def drawn_pair(key):
    base = jax.random.fold_in(key, 7)
    key_one, key_two = jax.random.split(base, 2)
    keys = jnp.clip(jax.random.normal(key_one, (SEQ, HEAD_DIM), jnp.float32), -6.0, 6.0)
    queries = jnp.clip(jax.random.normal(key_two, (SEQ, HEADS * HEAD_DIM), jnp.float32), -6.0, 6.0)
    return (queries, keys)


def draw_queries(key, part):
    return drawn_pair(key)[0].astype(jnp.bfloat16)


def draw_keys(key, part):
    return drawn_pair(key)[1].astype(jnp.bfloat16)


def level_of(stream_key, dims, cuts, smallest, top_value):
    gain = 1.0
    for dim, parts in cuts:
        heights = jax.random.uniform(jax.random.fold_in(jax.random.fold_in(stream_key, 6), dim), (parts,), jnp.float32, smallest / len(cuts), top_value / len(cuts))
        gain = gain * jnp.repeat(jnp.exp(heights), dims[dim] // parts).reshape((-1,) + (1,) * (len(dims) - 1 - dim))
    return gain


def profile(number_of, total, limit, lean):
    portions = [(1 << 20) // math.isqrt(grade ** lean) + 1 for grade in range(2, number_of + 1)]
    rest, counts = total - limit - (number_of - 1), [1] * (number_of - 1)
    while rest > 0:
        candidates = [i for i in range(number_of - 1) if counts[i] < limit]
        pool, left = sum([portions[i] for i in candidates]), rest
        for i in candidates:
            extra = min(limit - counts[i], max(1, left * portions[i] // pool), rest)
            counts[i] = counts[i] + extra
            rest = rest - extra
    return np.array([limit] + counts)


def ragged_sizes(rng, amount, total, bound, lean):
    if amount == 2:
        one = jax.random.randint(rng, (), max(1, total - bound), min(bound, total - 1) + 1)
        return jnp.stack([one, total - one])
    sizes = jnp.asarray(profile(amount, total, bound, lean), jnp.int32)
    couples = (amount - 1) // 2
    giver, receiver = sizes[1:1 + 2 * couples:2], sizes[2:2 + 2 * couples:2]
    slack = jnp.minimum(giver - 1, bound - receiver)
    passed = jax.random.randint(jax.random.fold_in(rng, 1), (couples,), 0, 1 << 20) % (slack + 1)
    sizes = sizes.at[1:1 + 2 * couples:2].set(giver - passed).at[2:2 + 2 * couples:2].set(receiver + passed)
    return sizes[jax.random.permutation(jax.random.fold_in(rng, 2), amount)]


def centred(key, dims, deviation, reach, cuts=(), kind=jnp.bfloat16):
    values = deviation * jax.random.normal(key, dims, jnp.float32)
    if cuts:
        values = values * level_of(key, dims, cuts, -0.22, 0.18)
    return jnp.clip(values, -reach, reach).astype(kind)


def setup_inputs(seed: int = 0, part: int = 0) -> dict:
    splits = jax.random.split(jax.random.key(seed), 5)
    part_splits = jax.random.split(jax.random.fold_in(splits[4], part), 5)
    return {
        "queries": draw_queries(jax.random.fold_in(jax.random.fold_in(splits[4], part), 71), part),
        "keys": draw_keys(jax.random.fold_in(jax.random.fold_in(splits[4], part), 71), part),
        "values": centred(part_splits[2], (SEQ, HEAD_DIM), 1.0, 6.0, ((0, 16),)),
        "doc_ids": jnp.searchsorted(jnp.cumsum(ragged_sizes(part_splits[3], DOCS, SEQ, LONGEST, 0)), jnp.arange(SEQ), side="right").astype(jnp.int32),
    }


def reference(queries, keys, values, doc_ids):
    score_scale = HEAD_DIM ** -0.5
    positions = jnp.arange(SEQ, dtype=jnp.int32)

    def query_block(block_index):
        start_row = (block_index * HALF).astype(jnp.int32)
        query_rows = lax.dynamic_slice_in_dim(queries, start_row, HALF, 0).reshape(HALF * HEADS, HEAD_DIM)
        scores = jnp.dot(query_rows, keys.T, preferred_element_type=jnp.float32) * score_scale
        query_place = jnp.repeat(start_row + jnp.arange(HALF, dtype=jnp.int32), HEADS)
        query_doc = jnp.repeat(lax.dynamic_slice_in_dim(doc_ids, start_row, HALF, 0), HEADS)
        visible = (positions[None, :] <= query_place[:, None]) & (doc_ids[None, :] == query_doc[:, None])
        row_max = jnp.max(jnp.where(visible, scores, -jnp.inf), axis=1)
        weights = jnp.where(visible, jnp.exp(scores - row_max[:, None]), 0.0)
        row_sum = jnp.sum(weights, axis=1)
        result = jnp.dot(weights.astype(jnp.bfloat16), values, preferred_element_type=jnp.float32) / row_sum[:, None]
        return result.astype(jnp.bfloat16).reshape(HALF, HEADS * HEAD_DIM)

    blocks = lax.map(query_block, jnp.arange(SEQ // HALF, dtype=jnp.int32))
    return blocks.reshape(SEQ, HEADS * HEAD_DIM)
```

```python
from functools import partial
import math

import jax
import jax.numpy as jnp
from jax import lax
from jax.experimental import pallas as pl
from jax.experimental.pallas import tpu as pltpu
from jax.sharding import PartitionSpec as P


LOW = -1e30
HIGH = 1e30
PAD_ROWS = 16
GROUP = 4

NT = (((1,), (1,)), ((), ()))


def scores_of(query, key):
    return lax.dot_general(query, key, NT, preferred_element_type=jnp.float32)


def ids_row(piece, rows):
    return piece[rows : rows + 1, :rows].astype(jnp.float32)


def attention_kernel(level_count, group, rows, heads, dim, *refs):
    place_ref, q_ref, own = refs[0], refs[1], refs[2]
    count = level_count * group - 1
    others = refs[3 : 3 + count]
    out_ref = refs[3 + count]
    acc, shift, vaug, every = refs[4 + count :]
    near, far = others[: group - 1], others[group - 1 :]
    place = place_ref[0]
    c2 = dim ** (-0.5) * math.log2(math.e)

    ones = jnp.ones((rows, dim), jnp.bfloat16)
    own_ids = ids_row(own, rows)
    own_ids_col = jnp.broadcast_to(own_ids, (dim, rows)).T[:, :1]
    first_id = own_ids[0, 0]
    u = lax.broadcasted_iota(jnp.int32, (rows, rows), 1)
    t = lax.broadcasted_iota(jnp.int32, (rows, rows), 0)
    visible = (u <= t) & (own_ids == own_ids_col)
    in_first = own_ids_col == first_id

    key_own = own[:rows, :dim]
    value_own = jnp.concatenate([own[:rows, dim:], ones], axis=1)
    for h in range(heads):
        s = scores_of(q_ref[:, h * dim : (h + 1) * dim], key_own)
        s = jnp.where(visible, s, LOW)
        m = jnp.max(s, axis=1, keepdims=True) * c2
        p = jnp.exp2(s * c2 - m)
        acc[h] = jnp.dot(p.astype(jnp.bfloat16), value_own, preferred_element_type=jnp.float32)
        shift[h] = jnp.broadcast_to(jnp.where(in_first, m, HIGH), (rows, dim))

    def group_step(pieces, valid):
        hidden = []
        for i, piece in enumerate(pieces):
            before = jnp.sum((ids_row(piece, rows) < first_id).astype(jnp.int32))
            hidden.append(jnp.where(valid[i], before, rows))
        fewest = hidden[0]
        for x in hidden[1:]:
            fewest = jnp.minimum(fewest, x)

        @pl.when(fewest < rows)
        def _():
            place_in = lax.broadcasted_iota(jnp.int32, (rows, dim), 0)
            for i, piece in enumerate(pieces):
                keep = place_in >= hidden[i]
                block = pl.ds(i * rows, rows)
                vaug[block, :dim] = jnp.where(keep, piece[:rows, dim:].astype(jnp.float32), 0.0).astype(jnp.bfloat16)
                vaug[block, dim:] = jnp.where(keep, 1.0, 0.0).astype(jnp.bfloat16)

            def head_step(h, _):
                query = q_ref[:, pl.ds(pl.multiple_of(h * dim, dim), dim)]
                m = jnp.concatenate([shift[h]] * (rows // dim), axis=1)
                ps = []
                for piece in pieces:
                    s = scores_of(query, piece[:rows, :dim])
                    ps.append(jnp.exp2(s * c2 - m).astype(jnp.bfloat16))
                acc[h] += jnp.dot(
                    jnp.concatenate(ps, axis=1),
                    vaug[: len(pieces) * rows, :],
                    preferred_element_type=jnp.float32,
                )
                return 0

            lax.fori_loop(0, heads, head_step, 0)

    index = place % group
    level = place // group
    if near:
        group_step(near, [(index ^ (i + 1)) < index for i in range(group - 1)])
    for k in range(1, level_count):
        group_step(far[(k - 1) * group : k * group], [level >= k] * group)

    worst = jnp.zeros((rows, dim), jnp.float32)
    for h in range(heads):
        total = acc[h]
        weight_sum = total[:, dim:]
        worst = jnp.maximum(worst, jnp.where(weight_sum < HIGH, 0.0, 1.0))
        out_ref[:, h * dim : (h + 1) * dim] = (total[:, :dim] / weight_sum).astype(jnp.bfloat16)

    @pl.when(jnp.max(worst) > 0.0)
    def _():
        for i, piece in enumerate((own, *others)):
            every[i] = piece[...]

        def head_step(h, _):
            query = q_ref[:, pl.ds(pl.multiple_of(h * dim, dim), dim)]

            def piece_step(i, state):
                top, weight_sum, weighted = state
                k, rest = i // group, i % group
                their_level, their_index = level - k, index ^ rest
                their_place = their_level * group + their_index
                piece = every[i]
                s = scores_of(query, piece[:rows, :dim]) * c2
                seen = (piece[rows : rows + 1, :rows].astype(jnp.float32) == own_ids_col) & (
                    their_place * rows + u <= place * rows + t
                ) & (their_level >= 0)
                s = jnp.where(seen, s, LOW)
                new_top = jnp.maximum(top, jnp.max(s, axis=1, keepdims=True))
                p = jnp.where(seen, jnp.exp2(s - new_top), 0.0)
                factor = jnp.exp2(top - new_top)
                weight_sum = weight_sum * factor + jnp.sum(p, axis=1, keepdims=True)
                weighted = weighted * factor + jnp.dot(
                    p.astype(jnp.bfloat16), piece[:rows, dim:], preferred_element_type=jnp.float32
                )
                return new_top, weight_sum, weighted

            _, weight_sum, weighted = lax.fori_loop(
                0,
                count + 1,
                piece_step,
                (
                    jnp.full((rows, 1), LOW, jnp.float32),
                    jnp.zeros((rows, 1), jnp.float32),
                    jnp.zeros((rows, dim), jnp.float32),
                ),
            )
            out_ref[:, pl.ds(pl.multiple_of(h * dim, dim), dim)] = (weighted / weight_sum).astype(jnp.bfloat16)
            return 0

        lax.fori_loop(0, heads, head_step, 0)


def on_device(ctx, queries, keys, values, doc_ids):
    rows, dim = keys.shape
    heads = queries.shape[1] // dim
    group = math.gcd(ctx, GROUP)
    level_count = ctx // group
    place = lax.axis_index("ctx").astype(jnp.int32)
    ids = jnp.pad(doc_ids.astype(jnp.bfloat16)[None, :], ((0, PAD_ROWS - 1), (0, 2 * dim - rows)))
    own = jnp.concatenate([jnp.concatenate([keys, values], axis=1), ids], axis=0)

    def shifted(x, k):
        return lax.ppermute(x, "ctx", [(i, i + k * group) for i in range(ctx - k * group)])

    def swapped(x, bit):
        return lax.ppermute(x, "ctx", [(i, i ^ bit) for i in range(ctx)])

    levels = [own] + [shifted(own, k) for k in range(1, level_count)]
    members = [levels]
    bit = group // 2
    pairs = [[x] for x in levels]
    bits = [1 << b for b in reversed(range(group.bit_length() - 1))]
    tables = [{0: x} for x in levels]
    for b in bits:
        for table in tables:
            for rest in list(table):
                table[rest | b] = swapped(table[rest], b)
    pieces = [table[rest] for table in tables for rest in range(group)]
    vmem = pl.BlockSpec(memory_space=pltpu.VMEM)
    return pl.pallas_call(
        partial(attention_kernel, level_count, group, rows, heads, dim),
        out_shape=jax.ShapeDtypeStruct((rows, heads * dim), jnp.bfloat16),
        in_specs=[pl.BlockSpec(memory_space=pltpu.SMEM)] + [vmem] * (1 + ctx),
        out_specs=vmem,
        scratch_shapes=[
            pltpu.VMEM((heads, rows, 2 * dim), jnp.float32),
            pltpu.VMEM((heads, rows, dim), jnp.float32),
            pltpu.VMEM((group * rows, 2 * dim), jnp.bfloat16),
            pltpu.VMEM((ctx, rows + PAD_ROWS, 2 * dim), jnp.bfloat16),
        ],
    )(place[None], queries, *pieces)


def solution(mesh):
    return jax.shard_map(
        partial(on_device, mesh.shape["ctx"]),
        mesh=mesh,
        in_specs=(
            P(("groups", "ctx"), None),
            P(("groups", "ctx"), None),
            P(("groups", "ctx"), None),
            P(("groups", "ctx")),
        ),
        out_specs=P(("groups", "ctx"), None),
        check_vma=False,
    )
```

```python
from functools import partial
import math

import jax
import jax.numpy as jnp
from jax import lax
from jax.experimental import pallas as pl
from jax.experimental.pallas import tpu as pltpu
from jax.sharding import PartitionSpec as P


LOW = -1e30
HIGH = 1e30
TAIL = 16
GROUP = 4

NT = (((1,), (1,)), ((), ()))
VMEM = pl.BlockSpec(memory_space=pltpu.VMEM)
SMEM = pl.BlockSpec(memory_space=pltpu.SMEM)
ANY = pl.BlockSpec(memory_space=pl.ANY)
PARAMS = pltpu.CompilerParams(vmem_limit_bytes=24 << 20)


def scores_of(key, query):
    return lax.dot_general(key, query, NT, preferred_element_type=jnp.float32)


def keys_of(piece, part, half, dim):
    return piece[:half, part * dim : (part + 1) * dim]


def ids_of(piece, half, dim):
    return piece[half + dim + 1 : half + dim + 2, :].astype(jnp.float32)


def pack_kernel(keys, values, ids, piece):
    rows, dim = keys.shape
    half = rows // 2
    piece[:half, :dim] = keys[:half]
    piece[:half, dim:] = keys[half:]
    piece[half : half + dim, :] = values[...].astype(jnp.float32).T.astype(jnp.bfloat16)
    row = lax.broadcasted_iota(jnp.int32, (TAIL, rows), 0)
    number = jnp.broadcast_to(ids[...].astype(jnp.float32), (TAIL, rows))
    tail = jnp.where(row == 0, 1.0, jnp.where(row == 1, number, 0.0))
    piece[half + dim :, :] = tail.astype(jnp.bfloat16)


def own_kernel(rows, heads, dim, q_ref, own, acc, shift):
    half = rows // 2
    c2 = dim ** (-0.5) * math.log2(math.e)
    ids = ids_of(own, half, dim)
    ids_col = jnp.broadcast_to(ids, (dim, rows)).T[:, :1]
    u = lax.broadcasted_iota(jnp.int32, (rows, rows), 0)
    t = lax.broadcasted_iota(jnp.int32, (rows, rows), 1)
    visible = (u <= t) & (ids_col == ids)
    in_first = ids == ids[0, 0]

    def head_step(h, _):
        query = q_ref[:, pl.ds(pl.multiple_of(h * dim, dim), dim)]
        s = jnp.concatenate([scores_of(keys_of(own, i, half, dim), query) for i in range(2)], axis=0)
        s = jnp.where(visible, s, LOW)
        m = jnp.max(s, axis=0, keepdims=True) * c2
        p = jnp.exp2(s * c2 - m).astype(jnp.bfloat16)
        acc[h] = jnp.dot(own[half:, :], p, preferred_element_type=jnp.float32)
        shift[h] = jnp.broadcast_to(jnp.where(in_first, m, HIGH), (8, rows))
        return 0

    lax.fori_loop(0, heads, head_step, 0, unroll=2)


def add_pieces(rows, heads, dim, q_ref, own, pieces, valid, acc, shift, masked):
    half = rows // 2
    c2 = dim ** (-0.5) * math.log2(math.e)
    first_id = ids_of(own, half, dim)[0, 0]
    hidden = []
    for i, piece in enumerate(pieces):
        before = jnp.sum((ids_of(piece, half, dim) < first_id).astype(jnp.int32))
        hidden.append(jnp.where(valid[i], before, rows))
    fewest = hidden[0]
    for x in hidden[1:]:
        fewest = jnp.minimum(fewest, x)

    @pl.when(fewest < rows)
    def _():
        lane = lax.broadcasted_iota(jnp.int32, (dim + TAIL, rows), 1)
        for i, piece in enumerate(pieces):
            keep = jnp.where(lane >= hidden[i], 1.0, 0.0).astype(jnp.bfloat16)
            masked[:, i * rows : (i + 1) * rows] = piece[half:, :] * keep

        def head_step(h, _):
            query = q_ref[:, pl.ds(pl.multiple_of(h * dim, dim), dim)]
            m = shift[h][:1]
            ps = []
            for piece in pieces:
                for i in range(2):
                    s = scores_of(keys_of(piece, i, half, dim), query)
                    ps.append(jnp.exp2(s * c2 - m).astype(jnp.bfloat16))
            acc[h] += jnp.dot(
                masked[:, : len(pieces) * rows],
                jnp.concatenate(ps, axis=0),
                preferred_element_type=jnp.float32,
            )
            return 0

        lax.fori_loop(0, heads, head_step, 0, unroll=2)


def validity(place, group, k):
    index, level = place % group, place // group
    if k == 0:
        return [(index ^ i) < index for i in range(1, group)]
    return [level >= k] * group


def step_kernel(rows, heads, dim, group, k, count, *refs):
    place_ref, q_ref, own = refs[:3]
    pieces = refs[3 : 3 + count]
    acc_in, shift, acc, masked = refs[3 + count :]
    add_pieces(rows, heads, dim, q_ref, own, pieces, validity(place_ref[0], group, k), acc, shift, masked)


def last_kernel(rows, heads, dim, group, k, count, total, *refs):
    place_ref, q_ref, own = refs[:3]
    pieces = refs[3 : 3 + count]
    every_piece = refs[3 + count : 3 + count + total]
    acc_in, shift, acc_out, out_ref, masked, every = refs[3 + count + total :]
    acc = acc_out
    half = rows // 2
    c2 = dim ** (-0.5) * math.log2(math.e)
    place = place_ref[0]
    if count:
        add_pieces(rows, heads, dim, q_ref, own, pieces, validity(place, group, k), acc, shift, masked)

    worst = jnp.zeros((1, rows), jnp.float32)
    for h in range(heads):
        sums = acc[h]
        weight_sum = sums[dim : dim + 1]
        worst = jnp.maximum(worst, jnp.where(weight_sum < HIGH, 0.0, 1.0))
        out_ref[:, h * dim : (h + 1) * dim] = (sums[:dim] / weight_sum).T.astype(jnp.bfloat16)

    @pl.when(jnp.max(worst) > 0.0)
    def _():
        for i, piece in enumerate(every_piece):
            pltpu.sync_copy(piece, every.at[i])
        index, level = place % group, place // group
        ids = ids_of(own, half, dim)
        u = lax.broadcasted_iota(jnp.int32, (rows, rows), 0)
        t = lax.broadcasted_iota(jnp.int32, (rows, rows), 1)

        def head_step(h, _):
            query = q_ref[:, pl.ds(pl.multiple_of(h * dim, dim), dim)]

            def piece_step(i, state):
                top, weighted = state
                k, rest = i // group, i % group
                their_level = level - k
                their_place = their_level * group + (index ^ rest)
                piece = every[i]
                s = jnp.concatenate([scores_of(keys_of(piece, j, half, dim), query) for j in range(2)], axis=0) * c2
                their_ids = piece[half + dim + 1 : half + dim + 2, :].astype(jnp.float32)
                their_col = jnp.broadcast_to(their_ids, (dim, rows)).T[:, :1]
                seen = (their_col == ids) & (their_place * rows + u <= place * rows + t) & (their_level >= 0)
                s = jnp.where(seen, s, LOW)
                new_top = jnp.maximum(top, jnp.max(s, axis=0, keepdims=True))
                p = jnp.where(seen, jnp.exp2(s - new_top), 0.0).astype(jnp.bfloat16)
                weighted = weighted * jnp.exp2(top - new_top) + jnp.dot(
                    piece[half:, :], p, preferred_element_type=jnp.float32
                )
                return new_top, weighted

            _, weighted = lax.fori_loop(
                0,
                total,
                piece_step,
                (jnp.full((1, rows), LOW, jnp.float32), jnp.zeros((dim + TAIL, rows), jnp.float32)),
            )
            part = (weighted[:dim] / weighted[dim : dim + 1]).T.astype(jnp.bfloat16)
            out_ref[:, pl.ds(pl.multiple_of(h * dim, dim), dim)] = part
            return 0

        lax.fori_loop(0, heads, head_step, 0)


def on_device(ctx, queries, keys, values, doc_ids):
    rows, dim = keys.shape
    heads = queries.shape[1] // dim
    group = math.gcd(ctx, GROUP)
    level_count = ctx // group
    place = lax.axis_index("ctx").astype(jnp.int32)[None]
    piece_shape = (rows // 2 + dim + TAIL, rows)
    own = pl.pallas_call(
        pack_kernel,
        out_shape=jax.ShapeDtypeStruct(piece_shape, jnp.bfloat16),
        in_specs=[VMEM] * 3,
        out_specs=VMEM,
        compiler_params=PARAMS,
        name="pack",
    )(keys, values, doc_ids[None])

    def shifted(x, k):
        return lax.ppermute(x, "ctx", [(i, i + k * group) for i in range(ctx - k * group)])

    def swapped(x, bit):
        return lax.ppermute(x, "ctx", [(i, i ^ bit) for i in range(ctx)])

    tables = [{0: own}] + [{0: shifted(own, k)} for k in range(1, level_count)]
    for bit in [1 << b for b in reversed(range(group.bit_length() - 1))]:
        for table in tables:
            for rest in list(table):
                table[rest | bit] = swapped(table[rest], bit)
    levels = [[table[rest] for rest in range(group)] for table in tables]

    acc_shape = jax.ShapeDtypeStruct((heads, dim + TAIL, rows), jnp.float32)
    shift_shape = jax.ShapeDtypeStruct((heads, 8, rows), jnp.float32)

    def cost(keys_seen):
        return pl.CostEstimate(
            flops=4 * rows * heads * dim * keys_seen,
            transcendentals=rows * heads * keys_seen,
            bytes_accessed=4 * rows * heads * dim,
        )

    acc, shift = pl.pallas_call(
        partial(own_kernel, rows, heads, dim),
        out_shape=(acc_shape, shift_shape),
        in_specs=[VMEM] * 2,
        out_specs=(VMEM, VMEM),
        compiler_params=PARAMS,
        cost_estimate=cost(rows),
        name="own_block",
    )(queries, own)
    every = [piece for level in levels for piece in level]
    for k, level in enumerate(levels):
        pieces = level[1:] if k == 0 else level
        count = len(pieces)
        masked = pltpu.VMEM((dim + TAIL, max(count, 1) * rows), jnp.bfloat16)
        if k < level_count - 1:
            acc = pl.pallas_call(
                partial(step_kernel, rows, heads, dim, group, k, count),
                out_shape=acc_shape,
                in_specs=[SMEM] + [VMEM] * (4 + count),
                out_specs=VMEM,
                scratch_shapes=[masked],
                input_output_aliases={3 + count: 0},
                compiler_params=PARAMS,
                cost_estimate=cost(count * rows),
                name=f"level_{k}",
            )(place, queries, own, *pieces, acc, shift)
        else:
            _, out = pl.pallas_call(
                partial(last_kernel, rows, heads, dim, group, k, count, len(every)),
                out_shape=(acc_shape, jax.ShapeDtypeStruct((rows, heads * dim), jnp.bfloat16)),
                in_specs=[SMEM] + [VMEM] * (2 + count) + [ANY] * len(every) + [VMEM] * 2,
                out_specs=(VMEM, VMEM),
                scratch_shapes=[masked, pltpu.VMEM((len(every), *piece_shape), jnp.bfloat16)],
                input_output_aliases={3 + count + len(every): 0},
                compiler_params=PARAMS,
                cost_estimate=cost(count * rows),
                name=f"level_{k}",
            )(place, queries, own, *pieces, *every, acc, shift)
    return out


def solution(mesh):
    return jax.shard_map(
        partial(on_device, mesh.shape["ctx"]),
        mesh=mesh,
        in_specs=(
            P(("groups", "ctx"), None),
            P(("groups", "ctx"), None),
            P(("groups", "ctx"), None),
            P(("groups", "ctx")),
        ),
        out_specs=P(("groups", "ctx"), None),
        check_vma=False,
    )
```

```python
from functools import partial
import math

import jax
import jax.numpy as jnp
from jax import lax
from jax.experimental import pallas as pl
from jax.experimental.pallas import tpu as pltpu
from jax.sharding import PartitionSpec as P


LOW = -1e30
HIGH = 1e30
TAIL = 16
UNROLL = 4
GROUP = 4

NT = (((1,), (1,)), ((), ()))
VMEM = pl.BlockSpec(memory_space=pltpu.VMEM)
SMEM = pl.BlockSpec(memory_space=pltpu.SMEM)
ANY = pl.BlockSpec(memory_space=pl.ANY)
PARAMS = pltpu.CompilerParams(vmem_limit_bytes=24 << 20)


def scores_of(key, query):
    return lax.dot_general(key, query, NT, preferred_element_type=jnp.float32)


def keys_of(piece, part, half, dim):
    return piece[:half, part * dim : (part + 1) * dim]


def ids_of(piece, half, dim):
    return piece[half + dim + 1 : half + dim + 2, :].astype(jnp.float32)


def pack_kernel(keys_hbm, values_hbm, ids_hbm, piece, keys, values, ids, sems):
    copies = [
        pltpu.make_async_copy(source, target, sems.at[i])
        for i, (source, target) in enumerate(((values_hbm, values), (keys_hbm, keys), (ids_hbm, ids)))
    ]
    for copy in copies:
        copy.start()
    rows, dim = keys.shape
    half = rows // 2
    copies[0].wait()
    piece[half : half + dim, :] = values[...].astype(jnp.float32).T.astype(jnp.bfloat16)
    copies[1].wait()
    piece[:half, :dim] = keys[:half]
    piece[:half, dim:] = keys[half:]
    copies[2].wait()
    row = lax.broadcasted_iota(jnp.int32, (TAIL, rows), 0)
    number = jnp.broadcast_to(ids[...].astype(jnp.float32), (TAIL, rows))
    tail = jnp.where(row == 0, 1.0, jnp.where(row == 1, number, 0.0))
    piece[half + dim :, :] = tail.astype(jnp.bfloat16)


def own_kernel(rows, heads, dim, q_ref, own, acc, shift):
    half = rows // 2
    c2 = dim ** (-0.5) * math.log2(math.e)
    ids = ids_of(own, half, dim)
    ids_col = jnp.broadcast_to(ids, (dim, rows)).T[:, :1]
    u = lax.broadcasted_iota(jnp.int32, (rows, rows), 0)
    t = lax.broadcasted_iota(jnp.int32, (rows, rows), 1)
    visible = (u <= t) & (ids_col == ids)
    in_first = ids == ids[0, 0]

    def head_step(h, _):
        query = q_ref[:, pl.ds(pl.multiple_of(h * dim, dim), dim)]
        s = jnp.concatenate([scores_of(keys_of(own, i, half, dim), query) for i in range(2)], axis=0)
        s = jnp.where(visible, s, LOW)
        m = jnp.max(s, axis=0, keepdims=True) * c2
        p = jnp.exp2(s * c2 - m).astype(jnp.bfloat16)
        acc[h] = jnp.dot(own[half:, :], p, preferred_element_type=jnp.float32)
        shift[h] = jnp.broadcast_to(jnp.where(in_first, m, HIGH), (8, rows))
        return 0

    lax.fori_loop(0, heads, head_step, 0, unroll=2)


def add_pieces(rows, heads, dim, q_ref, own, pieces, valid, acc, shift, masked):
    half = rows // 2
    c2 = dim ** (-0.5) * math.log2(math.e)
    first_id = ids_of(own, half, dim)[0, 0]
    hidden = []
    for i, piece in enumerate(pieces):
        before = jnp.sum((ids_of(piece, half, dim) < first_id).astype(jnp.int32))
        hidden.append(jnp.where(valid[i], before, rows))
    fewest = hidden[0]
    for x in hidden[1:]:
        fewest = jnp.minimum(fewest, x)

    @pl.when(fewest < rows)
    def _():
        lane = lax.broadcasted_iota(jnp.int32, (dim + TAIL, rows), 1)
        for i, piece in enumerate(pieces):
            keep = jnp.where(lane >= hidden[i], 1.0, 0.0).astype(jnp.bfloat16)
            masked[:, i * rows : (i + 1) * rows] = piece[half:, :] * keep

        def head_step(h, _):
            query = q_ref[:, pl.ds(pl.multiple_of(h * dim, dim), dim)]
            m = shift[h][:1]
            ps = []
            for piece in pieces:
                for i in range(2):
                    s = scores_of(keys_of(piece, i, half, dim), query)
                    ps.append(jnp.exp2(s * c2 - m).astype(jnp.bfloat16))
            acc[h] += jnp.dot(
                masked[:, : len(pieces) * rows],
                jnp.concatenate(ps, axis=0),
                preferred_element_type=jnp.float32,
            )
            return 0

        lax.fori_loop(0, heads, head_step, 0, unroll=UNROLL)


def validity(place, group, names):
    index, level = place % group, place // group
    return [(index ^ rest) < index if k == 0 else level >= k for k, rest in names]


def step_kernel(rows, heads, dim, group, names, *refs):
    count = len(names)
    place_ref, q_ref, own = refs[:3]
    pieces = refs[3 : 3 + count]
    _, shift, acc, masked = refs[3 + count :]
    add_pieces(rows, heads, dim, q_ref, own, pieces, validity(place_ref[0], group, names), acc, shift, masked)


def last_kernel(rows, heads, dim, group, names, total, *refs):
    count = len(names)
    place_ref, q_ref, own = refs[:3]
    pieces = refs[3 : 3 + count]
    every_piece = refs[3 + count : 3 + count + total]
    _, shift, acc_out, out_ref, masked, every = refs[3 + count + total :]
    acc = acc_out
    half = rows // 2
    c2 = dim ** (-0.5) * math.log2(math.e)
    place = place_ref[0]
    add_pieces(rows, heads, dim, q_ref, own, pieces, validity(place, group, names), acc, shift, masked)

    worst = jnp.zeros((1, rows), jnp.float32)
    for h in range(heads):
        sums = acc[h]
        weight_sum = sums[dim : dim + 1]
        worst = jnp.maximum(worst, jnp.where(weight_sum < HIGH, 0.0, 1.0))
        out_ref[:, h * dim : (h + 1) * dim] = (sums[:dim] / weight_sum).T.astype(jnp.bfloat16)

    @pl.when(jnp.max(worst) > 0.0)
    def _():
        for i, piece in enumerate(every_piece):
            pltpu.sync_copy(piece, every.at[i])
        index, level = place % group, place // group
        ids = ids_of(own, half, dim)
        u = lax.broadcasted_iota(jnp.int32, (rows, rows), 0)
        t = lax.broadcasted_iota(jnp.int32, (rows, rows), 1)

        def head_step(h, _):
            query = q_ref[:, pl.ds(pl.multiple_of(h * dim, dim), dim)]

            def piece_step(i, state):
                top, weighted = state
                k, rest = i // group, i % group
                their_level = level - k
                their_place = their_level * group + (index ^ rest)
                piece = every[i]
                s = jnp.concatenate([scores_of(keys_of(piece, j, half, dim), query) for j in range(2)], axis=0) * c2
                their_ids = piece[half + dim + 1 : half + dim + 2, :].astype(jnp.float32)
                their_col = jnp.broadcast_to(their_ids, (dim, rows)).T[:, :1]
                seen = (their_col == ids) & (their_place * rows + u <= place * rows + t) & (their_level >= 0)
                s = jnp.where(seen, s, LOW)
                new_top = jnp.maximum(top, jnp.max(s, axis=0, keepdims=True))
                p = jnp.where(seen, jnp.exp2(s - new_top), 0.0).astype(jnp.bfloat16)
                weighted = weighted * jnp.exp2(top - new_top) + jnp.dot(
                    piece[half:, :], p, preferred_element_type=jnp.float32
                )
                return new_top, weighted

            _, weighted = lax.fori_loop(
                0,
                total,
                piece_step,
                (jnp.full((1, rows), LOW, jnp.float32), jnp.zeros((dim + TAIL, rows), jnp.float32)),
            )
            part = (weighted[:dim] / weighted[dim : dim + 1]).T.astype(jnp.bfloat16)
            out_ref[:, pl.ds(pl.multiple_of(h * dim, dim), dim)] = part
            return 0

        lax.fori_loop(0, heads, head_step, 0)


def plan(ctx):
    group = math.gcd(ctx, GROUP)
    levels = ctx // group
    top = group // 2
    near = [(0, rest) for rest in range(1, group)]
    far = [
        [(k, half + rest) for rest in range(top)]
        for half in (0, top)
        for k in range(1, levels)
    ]
    kernels = [near] + [sum(far[i : i + 2], []) for i in range(0, len(far), 2)]
    order = [("send", (k, 0)) for k in range(1, levels)]
    order += [("send", (0, top)), ("send", (0, 1)), ("own", None)]
    order += [("send", x) for x in ((0, 3), (levels - 1, top), (1, top), (1, 1))]
    order += [("add", 0)]
    order += [("send", (k, top)) for k in range(2, levels - 1)]
    order += [("send", (k, 1)) for k in range(2, levels)]
    order += [("send", (1, 3)), ("add", 1)]
    order += [("send", (k, 3)) for k in range(2, levels)]
    order += [("add", i) for i in range(2, len(kernels))]
    return group, levels, kernels, order


def on_device(ctx, queries, keys, values, doc_ids):
    rows, dim = keys.shape
    heads = queries.shape[1] // dim
    group, levels, kernels, order = plan(ctx)
    top = group // 2
    place = lax.axis_index("ctx").astype(jnp.int32)[None]
    piece_shape = (rows // 2 + dim + TAIL, rows)
    piece_type = jax.ShapeDtypeStruct(piece_shape, jnp.bfloat16)
    acc_type = jax.ShapeDtypeStruct((heads, dim + TAIL, rows), jnp.float32)
    shift_type = jax.ShapeDtypeStruct((heads, 8, rows), jnp.float32)
    own = pl.pallas_call(
        pack_kernel,
        out_shape=piece_type,
        in_specs=[ANY] * 3,
        out_specs=VMEM,
        scratch_shapes=[
            pltpu.VMEM((rows, dim), jnp.bfloat16),
            pltpu.VMEM((rows, dim), jnp.bfloat16),
            pltpu.VMEM((1, rows), jnp.int32),
            pltpu.SemaphoreType.DMA((3,)),
        ],
        compiler_params=PARAMS,
        name="pack",
    )(keys, values, doc_ids[None])

    def cost(keys_seen):
        return pl.CostEstimate(
            flops=4 * rows * heads * dim * keys_seen,
            transcendentals=rows * heads * keys_seen,
            bytes_accessed=4 * rows * heads * dim,
        )

    pieces = {(0, 0): own}

    def send(which):
        k, rest = which
        if k and (rest == 0 or which == (levels - 1, top)):
            source, pairs = (0, rest), [(i, (i + k * group) % ctx) for i in range(ctx)]
        else:
            bit = top if rest == top else 1
            source, pairs = (k, rest ^ bit), [(i, i ^ bit) for i in range(ctx)]
        pieces[which] = lax.ppermute(pieces[source], "ctx", pairs)

    for what, which in order:
        if what == "send":
            send(which)
        elif what == "own":
            acc, shift = pl.pallas_call(
                partial(own_kernel, rows, heads, dim),
                out_shape=(acc_type, shift_type),
                in_specs=[VMEM] * 2,
                out_specs=(VMEM, VMEM),
                compiler_params=PARAMS,
                cost_estimate=cost(rows),
                name="own_block",
            )(queries, own)
        else:
            names = kernels[which]
            count = len(names)
            given = [pieces[x] for x in names]
            masked = pltpu.VMEM((dim + TAIL, count * rows), jnp.bfloat16)
            if which < len(kernels) - 1:
                acc = pl.pallas_call(
                    partial(step_kernel, rows, heads, dim, group, names),
                    out_shape=acc_type,
                    in_specs=[SMEM] + [VMEM] * (4 + count),
                    out_specs=VMEM,
                    scratch_shapes=[masked],
                    input_output_aliases={3 + count: 0},
                    compiler_params=PARAMS,
                    cost_estimate=cost(count * rows),
                )(place, queries, own, *given, acc, shift)
            else:
                every = [pieces[k, rest] for k in range(levels) for rest in range(group)]
                _, out = pl.pallas_call(
                    partial(last_kernel, rows, heads, dim, group, names, len(every)),
                    out_shape=(acc_type, jax.ShapeDtypeStruct((rows, heads * dim), jnp.bfloat16)),
                    in_specs=[SMEM] + [VMEM] * (2 + count) + [ANY] * len(every) + [VMEM] * 2,
                    out_specs=(VMEM, VMEM),
                    scratch_shapes=[masked, pltpu.VMEM((len(every), *piece_shape), jnp.bfloat16)],
                    input_output_aliases={3 + count + len(every): 0},
                    compiler_params=PARAMS,
                    cost_estimate=cost(count * rows),
                )(place, queries, own, *given, *every, acc, shift)
    return out


def solution(mesh):
    ctx = mesh.shape["ctx"]

    def body(*arrays):
        return on_device(ctx, *arrays)

    return jax.shard_map(
        body,
        mesh=mesh,
        in_specs=(
            P(("groups", "ctx"), None),
            P(("groups", "ctx"), None),
            P(("groups", "ctx"), None),
            P(("groups", "ctx")),
        ),
        out_specs=P(("groups", "ctx"), None),
        check_vma=False,
    )
```
